32 devices in a mesh: doc: 32 (over z, y, x, core).
Axes of the slice: x: 2, y: 2, z: 4, core: 2. Of those that a mesh axis runs over, the one named last changes fastest.
Arguments:
- documents: bfloat16 [24576, 1024], P('doc'), may hold values from -64 to 64
- labels: bfloat16 [24576, 128], P('doc'), may hold values from -16 to 16
- skeleton: bfloat16 [8192, 1024], P('doc'), may hold values from -64 to 64
- transfer: float32 [2, 4, 256, 256], replicated, may hold values from 0 to 1.5, as said below
- near_peer: int32 [32, 2], P('doc'), may hold values from 0 to 1
- near_live: int32 [32, 2], P('doc'), may hold values 0 or 1
- couple_peer: int32 [32, 3, 2], P('doc'), may hold values from 0 to 1
- couple_live: int32 [32, 3, 2], P('doc'), may hold values 0 or 1
Outputs:
- scores: float32 [24576, 128], P('doc')
The draws below stay inside these ranges and needn't reach their ends.
Inputs may be any that keep to these rules, and one draw needn't show every extreme that they name: `transfer`: entries are not negative.
All inputs are finite; a program needn't handle non-finite values. No bound on the sum of `near_live` or of `couple_live` on one device may be relied on, other than what follows from the above.
Results may differ from the reference program's by a relative error of at most 0.003.
Values may be sent and summed in bfloat16 or wider, within the bound.
No kernel may reach another device: no remote copies, remote signals or barrier semaphores. Data moves between devices by JAX's collectives and lax.ppermute only.
A program may use at most 64 MiB of HBM per device.

```python
import math
import jax
import jax.numpy as jnp
from jax import lax

D = 1024
C = 128
R = 256
LEV = 2
SLOTS = 2
DOC_DEV = 768
DOCS = 24576
POINTS = 8192
N_DOC = 32


center_count = 8


center_weight = 0.26


def cluster_centers(key):
    return jnp.clip(jax.random.normal(jax.random.fold_in(key, 5), (center_count, D), jnp.float32), -4.0, 4.0)


def block_mix(key):
    first_key, second_key = jax.random.split(jax.random.fold_in(key, 7))
    block_total = DOCS // DOC_DEV
    first_cluster = jax.random.randint(first_key, (block_total,), 0, center_count)
    second_cluster = (first_cluster + jax.random.randint(second_key, (block_total,), 1, center_count)) % center_count
    return (first_cluster, second_cluster)


def row_clusters(key, salt, row_count, rows_per_block):
    choose_key, any_key = jax.random.split(jax.random.fold_in(key, salt))
    pick_value = jax.random.randint(choose_key, (row_count,), 0, 4)
    anywhere = jax.random.randint(any_key, (row_count,), 0, center_count)
    block_place = jnp.arange(row_count, dtype=jnp.int32) // rows_per_block
    first_cluster, second_cluster = block_mix(key)
    return jnp.where(pick_value < 2, first_cluster[block_place], jnp.where(pick_value == 2, second_cluster[block_place], anywhere))


def spread_rows(key, salt, row_count, rows_per_block, col_count):
    first_key, second_key = jax.random.split(jax.random.fold_in(key, salt), 2)
    centers = cluster_centers(key)
    clusters = row_clusters(key, salt + 100, row_count, rows_per_block)
    base_values = jnp.clip(jax.random.normal(first_key, (row_count, col_count), jnp.float32), -6.0, 6.0)
    base_values = base_values + center_weight * centers[clusters]
    row_scale = jnp.exp(jax.random.uniform(second_key, (row_count, 1), jnp.float32, 0.0, math.log(10.0)))
    return jnp.clip(base_values * row_scale, -64.0, 64.0)


def draw_documents(key, part):
    return spread_rows(key, 11, DOCS, DOC_DEV, D).astype(jnp.bfloat16)


def draw_skeleton(key, part):
    return spread_rows(key, 23, POINTS, R, D).astype(jnp.bfloat16)


def draw_labels(key, part):
    base_key = jax.random.fold_in(key, 47)
    noise_key = jax.random.fold_in(base_key, 0)
    ampl_key = jax.random.fold_in(base_key, 1)
    wave_key = jax.random.fold_in(base_key, 2)
    phase_key = jax.random.fold_in(base_key, 3)
    offset_key = jax.random.fold_in(base_key, 5)
    block_place = (jnp.arange(DOCS, dtype=jnp.int32) // DOC_DEV).astype(jnp.float32)
    amplitudes = 1.5 * jax.random.normal(ampl_key, (3, C), jnp.float32)
    wavelengths = jnp.exp(jax.random.uniform(wave_key, (3, C), jnp.float32, math.log(16.0), math.log(64.0)))
    phases = jax.random.uniform(phase_key, (3, C), jnp.float32, -math.pi, math.pi)
    smooth_part = jnp.zeros((DOCS, C), jnp.float32)
    for term_index in range(3):
        angle_now = 2.0 * math.pi * block_place[:, None] / wavelengths[term_index][None, :] + phases[term_index][None, :]
        smooth_part = smooth_part + amplitudes[term_index][None, :] * jnp.cos(angle_now)
    cluster_offsets = jax.random.uniform(offset_key, (center_count, C), jnp.float32, -8.0, 8.0)
    doc_clusters = row_clusters(key, 111, DOCS, DOC_DEV)
    smooth_part = smooth_part + cluster_offsets[doc_clusters]
    noise_part = jnp.clip(3.0 * jax.random.normal(noise_key, (DOCS, C), jnp.float32), -15.0, 15.0)
    return jnp.clip(noise_part + smooth_part, -16.0, 16.0).astype(jnp.bfloat16)


def draw_transfer(key, part):
    first_key, second_key = jax.random.split(jax.random.fold_in(key, 37))
    diag_values = jnp.exp(jax.random.uniform(first_key, (LEV, 4, R), jnp.float32, math.log(0.5), math.log(1.5)))
    spread_values = jax.random.uniform(second_key, (LEV, 4, R, R), jnp.float32, 0.0, 0.6 / R)
    eye_mask = jnp.eye(R, dtype=jnp.float32)
    return spread_values * (1.0 - eye_mask) + diag_values[:, :, :, None] * eye_mask


def touch_ends(drawn, own_key, least, largest):
    longest = drawn.shape.index(max(drawn.shape))
    spots = []
    for shift in (0, 1):
        where = [jax.random.randint(jax.random.fold_in(own_key, axis), (), 0, length) for axis, length in enumerate(drawn.shape)]
        where[longest] = (where[longest] + shift) % drawn.shape[longest]
        spots.append(tuple(where))
    return drawn.at[spots[0]].set(least).at[spots[1]].set(largest)


def setup_inputs(seed: int = 0) -> dict:
    splits = jax.random.split(jax.random.key(seed), 9)
    documents = draw_documents(jax.random.fold_in(splits[8], 71), 0)
    labels = draw_labels(jax.random.fold_in(splits[8], 71), 0)
    skeleton = draw_skeleton(jax.random.fold_in(splits[8], 71), 0)
    transfer = draw_transfer(jax.random.fold_in(splits[8], 71), 0)
    near_peer = touch_ends(jax.random.randint(splits[4], (N_DOC, SLOTS), 0, 2), jax.random.fold_in(splits[4], 1), 0, 1).astype(jnp.int32)
    near_live = touch_ends((jax.random.randint(splits[5], (N_DOC, SLOTS), 0, 4) < 3).astype(jnp.int32), jax.random.fold_in(splits[5], 1), 0, 1)
    couple_peer = touch_ends(jax.random.randint(splits[6], (N_DOC, LEV + 1, SLOTS), 0, 2), jax.random.fold_in(splits[6], 1), 0, 1).astype(jnp.int32)
    couple_live = touch_ends((jax.random.randint(splits[7], (N_DOC, LEV + 1, SLOTS), 0, 4) < 3).astype(jnp.int32), jax.random.fold_in(splits[7], 1), 0, 1)
    return {"documents": documents, "labels": labels, "skeleton": skeleton, "transfer": transfer, "near_peer": near_peer, "near_live": near_live, "couple_peer": couple_peer, "couple_live": couple_live}


eps_value = 1e-06
far_gain = 64.0
contract_cols = (((1,), (1,)), ((), ()))

def normalize(row_block):
    widened = row_block.astype(jnp.float32)
    inv_scale = lax.rsqrt(lax.optimization_barrier(jnp.mean(widened * widened, axis=-1, keepdims=True)) + eps_value)
    return (widened * inv_scale).astype(jnp.bfloat16)

def square_sums(row_block):
    widened = row_block.astype(jnp.float32)
    return lax.optimization_barrier(jnp.sum(widened * widened, axis=1))

def kernel_tile(left_rows, left_sq, right_rows, right_sq):
    cross_dot = lax.dot_general(left_rows, right_rows, contract_cols, preferred_element_type=jnp.float32)
    feature_width = left_rows.shape[1]
    exponent = (2.0 * feature_width - (left_sq[:, None] + right_sq[None, :] - 2.0 * cross_dot)) / (2.0 * math.sqrt(feature_width))
    return jnp.exp(exponent)

def side_counts(peer_codes, live_flags):
    before_count = lax.optimization_barrier(jnp.sum(live_flags * (peer_codes == 0).astype(jnp.int32), axis=-1))
    after_count = lax.optimization_barrier(jnp.sum(live_flags * (peer_codes == 1).astype(jnp.int32), axis=-1))
    return (before_count, after_count)

def reference(documents, labels, skeleton, transfer, near_peer, near_live, couple_peer, couple_live):
    highest = lax.Precision.HIGHEST
    block_count = N_DOC
    docs_flat = normalize(documents)
    docs_norm = docs_flat.reshape(block_count, DOC_DEV, D)
    docs_sq = square_sums(docs_flat).reshape(block_count, DOC_DEV)
    label_blocks = labels.reshape(block_count, DOC_DEV, C)
    points_flat = normalize(skeleton)
    points_norm = points_flat.reshape(block_count, R, D)
    points_sq = square_sums(points_flat).reshape(block_count, R)
    block_ids = jnp.arange(block_count, dtype=jnp.int32)
    near_before, near_after = side_counts(near_peer, near_live)
    near_before = near_before * (block_ids >= 1).astype(jnp.int32)
    near_after = near_after * (block_ids <= block_count - 2).astype(jnp.int32)
    diagonal = jnp.arange(DOC_DEV)[:, None] == jnp.arange(DOC_DEV)[None, :]

    def near_block(block_id):
        mine_rows = docs_norm[block_id]
        mine_sq = docs_sq[block_id]
        own_tile = jnp.where(diagonal, 0.0, kernel_tile(mine_rows, mine_sq, mine_rows, mine_sq)).astype(jnp.bfloat16)
        near_num = jnp.dot(own_tile, label_blocks[block_id], preferred_element_type=jnp.float32)
        near_den = lax.optimization_barrier(jnp.sum(own_tile.astype(jnp.float32), axis=1))
        partners = (jnp.maximum(block_id - 1, 0), jnp.minimum(block_id + 1, block_count - 1))
        tallies = (near_before[block_id], near_after[block_id])
        for partner, tally_count in zip(partners, tallies):
            pair_tile = kernel_tile(mine_rows, mine_sq, docs_norm[partner], docs_sq[partner]).astype(jnp.bfloat16)
            weight = tally_count.astype(jnp.float32)
            near_num = near_num + weight * jnp.dot(pair_tile, label_blocks[partner], preferred_element_type=jnp.float32)
            near_den = near_den + weight * lax.optimization_barrier(jnp.sum(pair_tile.astype(jnp.float32), axis=1))
        leaf_kernel = kernel_tile(mine_rows, mine_sq, points_norm[block_id], points_sq[block_id]).astype(jnp.bfloat16)
        return (near_num, near_den, leaf_kernel)
    near_num, near_den, leaf_kernel = lax.map(near_block, block_ids)
    kernel_wide = leaf_kernel.astype(jnp.float32)
    leaf_num = jnp.einsum('bir,bic->brc', kernel_wide, label_blocks.astype(jnp.float32), precision=highest) / DOC_DEV
    leaf_den = lax.optimization_barrier(jnp.sum(kernel_wide, axis=1)) / DOC_DEV
    tier_weights = [(leaf_num, leaf_den)]
    node_num, node_den = (leaf_num, leaf_den)
    for height in range(1, LEV + 1):
        grouped_num = node_num.reshape(-1, 4, R, C)
        grouped_den = node_den.reshape(-1, 4, R)
        lifted_num = 0.25 * jnp.einsum('crs,kcrm->kcsm', transfer[height - 1], grouped_num, precision=highest)
        lifted_den = 0.25 * jnp.einsum('crs,kcr->kcs', transfer[height - 1], grouped_den, precision=highest)
        node_num = lifted_num[:, 0] + lifted_num[:, 1] + (lifted_num[:, 2] + lifted_num[:, 3])
        node_den = lifted_den[:, 0] + lifted_den[:, 1] + (lifted_den[:, 2] + lifted_den[:, 3])
        tier_weights.append((node_num, node_den))
    couple_before, couple_after = side_counts(couple_peer, couple_live)
    couplings = []
    for height in range(LEV + 1):
        stride = 4 ** height
        sent_num = tier_weights[height][0].astype(jnp.bfloat16)
        sent_den = tier_weights[height][1].astype(jnp.bfloat16)
        before_tally = couple_before[:, height] * (block_ids >= stride).astype(jnp.int32)
        after_tally = couple_after[:, height] * (block_ids <= block_count - 1 - stride).astype(jnp.int32)

        def couple_block(block_id):
            total_num = jnp.zeros((R, C), jnp.float32)
            total_den = jnp.zeros((R,), jnp.float32)
            partners = (jnp.maximum(block_id - stride, 0), jnp.minimum(block_id + stride, block_count - 1))
            tallies = (before_tally[block_id], after_tally[block_id])
            for partner, tally_count in zip(partners, tallies):
                pair_kernel = kernel_tile(points_norm[block_id], points_sq[block_id], points_norm[partner], points_sq[partner]).astype(jnp.bfloat16)
                node_id = partner // stride
                weight = tally_count.astype(jnp.float32)
                total_num = total_num + weight * jnp.dot(pair_kernel, sent_num[node_id], preferred_element_type=jnp.float32)
                total_den = total_den + weight * jnp.dot(pair_kernel, sent_den[node_id], preferred_element_type=jnp.float32)
            return (total_num / R, total_den / R)
        couplings.append(lax.map(couple_block, block_ids))
    down_num, down_den = couplings[LEV]
    for height in range(LEV, 0, -1):
        child_slot = block_ids // 4 ** (height - 1) % 4
        transfer_mat = transfer[height - 1][child_slot]
        down_num = couplings[height - 1][0] + jnp.einsum('brs,bsc->brc', transfer_mat, down_num, precision=highest)
        down_den = couplings[height - 1][1] + jnp.einsum('brs,bs->br', transfer_mat, down_den, precision=highest)
    far_num = far_gain / R * jnp.einsum('bir,brc->bic', kernel_wide, down_num, precision=highest)
    far_den = far_gain / R * jnp.einsum('bir,br->bi', kernel_wide, down_den, precision=highest)
    scores = (near_num + far_num) / (near_den + far_den)[:, :, None]
    return scores.reshape(block_count * DOC_DEV, C)
```

```python
import functools
import math

import jax
import jax.numpy as jnp
from jax import lax
from jax.experimental import pallas as pl
from jax.experimental.pallas import tpu as pltpu
from jax.sharding import PartitionSpec as P

f32 = jnp.float32
bf16 = jnp.bfloat16
eps_value = 1e-06
far_gain = 64.0
NN = (((1,), (0,)), ((), ()))
NT = (((1,), (1,)), ((), ()))
VMEM = pltpu.VMEM
SMEM = pltpu.SMEM


def shift_by(value, axis, by):
    devices = lax.axis_size(axis)
    pairs = [(i, i + by) for i in range(devices) if 0 <= i + by < devices]
    return lax.ppermute(value, axis, pairs)


def partner(block, axis, bit):
    count = lax.axis_size(axis)
    route = []
    for low in range(count):
        high = low | 1 << bit
        if high != low and high < count:
            route += [(low, high), (high, low)]
    return lax.ppermute(block, axis, route)


def swap(value, axis, by):
    count = lax.axis_size(axis)
    if count <= 2 * by:
        pairs = []
        for i in range(count - by):
            pairs += [(i, i + by), (i + by, i)]
        both = lax.ppermute(value, axis, pairs)
        return both, both
    return shift_by(value, axis, by), shift_by(value, axis, -by)


def dot(left, right, dims):
    return lax.dot_general(left, right, dims, preferred_element_type=f32)


def halves(value):
    high = value.astype(bf16)
    return high, (value - high.astype(f32)).astype(bf16)


def dot_wide(left, right, dims):
    left_high, left_low = halves(left)
    right_high, right_low = halves(right)
    return dot(left_high, right_high, dims) + (
        dot(left_high, right_low, dims) + dot(left_low, right_high, dims)
    )


def normalized(rows):
    wide = rows.astype(f32)
    inv_scale = lax.rsqrt(jnp.mean(wide * wide, axis=-1, keepdims=True) + eps_value)
    return (wide * inv_scale).astype(bf16)


def offsets(rows):
    width = rows.shape[1]
    wide = rows.astype(f32)
    total = jnp.sum(wide * wide, axis=1, keepdims=True)
    return (width - total) * (math.log2(math.e) / (2.0 * math.sqrt(width)))


def as_row(column):
    return jnp.transpose(jnp.broadcast_to(column, (column.shape[0], 128)))[0:8]


def as_column(row):
    return jnp.transpose(jnp.broadcast_to(row[0:1], (128, row.shape[1])))[:, 0:1]


def tile(left, left_column, right, right_row):
    width = left.shape[1]
    cross = dot(left, right, NT)
    return jnp.exp2(cross * (math.log2(math.e) / math.sqrt(width)) + (left_column + right_row[0:1]))


def padded(value):
    rows = value.shape[0]
    extra = -rows % 16
    if extra:
        value = jnp.concatenate([value, jnp.zeros((extra, value.shape[1]), value.dtype)], axis=0)
    return value.astype(bf16)


def labels_across(labels):
    cols = labels.shape[1]
    across = jnp.transpose(labels.astype(f32))
    ones = (lax.broadcasted_iota(jnp.int32, (16, labels.shape[0]), 0) == 0).astype(f32)
    return jnp.concatenate([across, ones], axis=0).astype(bf16)


def count(peer_ref, live_ref, at, code):
    total = jnp.int32(0)
    for slot in range(peer_ref.shape[-1]):
        where = at + (slot,)
        total = total + live_ref[where] * (peer_ref[where] == code).astype(jnp.int32)
    return total


def tally(peer_ref, live_ref, at, code, exists):
    return (count(peer_ref, live_ref, at, code) * exists.astype(jnp.int32)).astype(f32)


def pack_kernel(docs_ref, labels_ref, pack_ref, row_ref):
    width = docs_ref.shape[1]
    rows = normalized(docs_ref[...])
    pack_ref[:, :width] = rows
    pack_ref[:, width:] = labels_ref[...]
    row_ref[...] = as_row(offsets(rows))


def leaf_kernel(blocks, place_ref, skeleton_ref, pack_ref, row_ref, move_ref, points_ref, prow_ref, leaf_ref, across_ref, lifted_ref):
    rank, width = skeleton_ref.shape
    docs = pack_ref.shape[0]
    points = normalized(skeleton_ref[...])
    points_ref[0:rank] = points
    prow = as_row(offsets(points))
    prow_ref[...] = prow
    across = labels_across(pack_ref[:, width:])
    across_ref[...] = across
    leaf = tile(pack_ref[:, :width], as_column(row_ref[...]), points, prow).astype(bf16)
    leaf_ref[...] = leaf
    node = dot(across, leaf, NN) * (1.0 / docs)
    sent = node.astype(bf16)
    tall = sent.shape[0] // blocks
    for q in range(blocks):
        points_ref[rank : rank + tall, q * rank : (q + 1) * rank] = sent[q * tall : (q + 1) * tall]
    if blocks * rank < width:
        points_ref[rank : rank + tall, blocks * rank :] = jnp.zeros((tall, width - blocks * rank), bf16)
    lifted_ref[...] = 0.25 * dot_wide(node[0 : lifted_ref.shape[0]], move_ref[0, 0], NN)


def own_kernel(pack_ref, row_ref, across_ref, out_ref):
    docs = pack_ref.shape[0]
    width = pack_ref.shape[1] - across_ref.shape[0] + 16
    step = 256
    column = as_column(row_ref[...])
    total = jnp.zeros((across_ref.shape[0], docs), f32)
    for start in range(0, docs, step):
        some = tile(
            pack_ref[start : start + step, :width],
            column[start : start + step],
            pack_ref[:, :width],
            row_ref[...],
        )
        diagonal = (
            lax.broadcasted_iota(jnp.int32, some.shape, 0) + start
            == lax.broadcasted_iota(jnp.int32, some.shape, 1)
        )
        some = jnp.where(diagonal, 0.0, some).astype(bf16)
        total = total + dot(across_ref[:, start : start + step], some, NN)
    out_ref[...] = total[0 : out_ref.shape[0]]


def pair_kernel(pack_ref, row_ref, across_ref, other_ref, mine_ref, give_ref):
    docs = pack_ref.shape[0]
    width = pack_ref.shape[1] - across_ref.shape[0] + 16
    step = 256
    kept = mine_ref.shape[0]
    column = as_column(row_ref[...])
    other_row = as_row(offsets(other_ref[:, :width]))
    other_across = labels_across(other_ref[:, width:])
    total = jnp.zeros((across_ref.shape[0], docs), f32)
    for start in range(0, docs, step):
        some = tile(
            pack_ref[start : start + step, :width],
            column[start : start + step],
            other_ref[:, :width],
            other_row,
        ).astype(bf16)
        total = total + dot(across_ref[:, start : start + step], some, NN)
        mine_ref[:, start : start + step] = dot(other_across, some, NT)[0:kept]
    give_ref[...] = total[0:kept]


def gram_kernel(points_ref, prow_ref, other_ref, out_ref):
    rank = other_ref.shape[0]
    other = normalized(other_ref[...])
    out_ref[...] = tile(
        points_ref[0:rank], as_column(prow_ref[...]), other, as_row(offsets(other))
    ).astype(bf16)


def unpack_sent(points_ref, rank, blocks):
    return jnp.concatenate(
        [points_ref[rank:, q * rank : (q + 1) * rank] for q in range(blocks)], axis=0
    )


def leaf_couple_kernel(blocks, points_ref, prow_ref, other_ref, mine_ref, give_ref):
    rank = prow_ref.shape[1]
    kept = mine_ref.shape[0]
    other = other_ref[0:rank]
    gram = tile(
        points_ref[0:rank], as_column(prow_ref[...]), other, as_row(offsets(other))
    ).astype(bf16)
    mine_ref[...] = dot(unpack_sent(other_ref, rank, blocks), gram, NT)[0:kept]
    give_ref[...] = dot(unpack_sent(points_ref, rank, blocks), gram, NN)[0:kept]


def couple_kernel(gram_ref, sent_ref, other_ref, mine_ref, give_ref):
    kept = mine_ref.shape[0]
    gram = gram_ref[...]
    mine_ref[...] = dot(other_ref[...], gram, NT)[0:kept]
    give_ref[...] = dot(sent_ref[...], gram, NN)[0:kept]


def lift_kernel(place_ref, mine_ref, other_ref, move_ref, sent_ref, lifted_ref):
    node = mine_ref[...] + other_ref[...]
    sent_ref[...] = padded(node)
    lifted_ref[...] = 0.25 * dot_wide(node, move_ref[0, 0], NN)


def top_kernel(mine_ref, other_ref, sent_ref):
    sent_ref[...] = padded(mine_ref[...] + other_ref[...])


def far_kernel(
    size,
    place_ref,
    near_peer_ref,
    near_live_ref,
    peer_ref,
    live_ref,
    move_low_ref,
    move_high_ref,
    gram_ref,
    back_ref,
    top_before_ref,
    top_after_ref,
    mid_mine_ref,
    mid_give_ref,
    low_mine_ref,
    low_give_ref,
    leaf_ref,
    own_ref,
    pair_ref,
    out_ref,
):
    me = place_ref[0]
    rank = gram_ref.shape[0]
    kept = mid_mine_ref.shape[0]

    def sides(level):
        stride = 4**level
        before = tally(peer_ref, live_ref, (0, level), 0, me >= stride)
        after = tally(peer_ref, live_ref, (0, level), 1, me <= size - 1 - stride)
        return before, after

    scale = 1.0 / rank
    before, after = sides(2)
    down = (
        after * dot(top_after_ref[...], gram_ref[...], NT)
        + before * dot(top_before_ref[...], back_ref[...], NN)
    )[0:kept] * scale
    before, after = sides(1)
    far = (before * mid_mine_ref[...] + after * mid_give_ref[...]) * scale
    down = far + dot_wide(down, move_high_ref[0, 0], NT)
    before, after = sides(0)
    far = (after * low_mine_ref[...] + before * low_give_ref[...]) * scale
    down = far + dot_wide(down, move_low_ref[0, 0], NT)
    high, low = halves(down)
    leaf = leaf_ref[...]
    far = (far_gain / rank) * (dot(high, leaf, NT) + dot(low, leaf, NT))
    before = tally(near_peer_ref, near_live_ref, (0,), 0, me >= 1)
    out_ref[...] = own_ref[...] + before * pair_ref[...] + far


def score_kernel(size, place_ref, near_peer_ref, near_live_ref, part_ref, give_ref, out_ref):
    cols = out_ref.shape[1]
    after = tally(near_peer_ref, near_live_ref, (0,), 1, place_ref[0] <= size - 2)
    total = part_ref[...] + after * give_ref[...]
    out_ref[...] = jnp.transpose(total[0:cols] / total[cols : cols + 1])


def vmem(count):
    return [pl.BlockSpec(memory_space=VMEM)] * count


def call(body, name, outs, ins, flops=0):
    moved = sum(math.prod(o.shape) * o.dtype.itemsize for o in outs)
    moved += sum(math.prod(i.shape) * i.dtype.itemsize for i in ins)
    return pl.pallas_call(
        body,
        name=name,
        out_shape=outs,
        in_specs=vmem(len(ins)),
        out_specs=vmem(len(outs)),
        cost_estimate=pl.CostEstimate(flops=flops, bytes_accessed=moved, transcendentals=0),
    )(*ins)


def shape(rows, cols, dtype=f32):
    return jax.ShapeDtypeStruct((rows, cols), dtype)


def local(documents, labels, skeleton, transfer, near_peer, near_live, couple_peer, couple_live):
    size = lax.axis_size("doc")
    place = jnp.reshape(lax.axis_index("doc"), (1,)).astype(jnp.int32)
    docs, width = documents.shape
    cols = labels.shape[1]
    rank = skeleton.shape[0]
    kept = cols + 8
    tall = cols + 16
    blocks = max(b for b in range(1, width // rank + 1) if tall % (16 * b) == 0)
    step = 256

    def full(value):
        return pl.BlockSpec(value.shape, lambda i, p: (0,) * value.ndim)

    def move(level):
        return pl.BlockSpec((1, 1, rank, rank), lambda i, p: (level, (p[0] >> (2 * level)) & 3, 0, 0))

    def placed_call(body, name, outs, ins, specs, flops=0):
        return pl.pallas_call(
            body,
            name=name,
            out_shape=outs,
            grid_spec=pltpu.PrefetchScalarGridSpec(
                num_scalar_prefetch=1,
                grid=(1,),
                in_specs=specs,
                out_specs=[full(o) for o in outs] if isinstance(outs, list) else full(outs),
            ),
            cost_estimate=pl.CostEstimate(flops=flops, bytes_accessed=4 << 20, transcendentals=0),
        )(place, *ins)

    pack, row = pl.pallas_call(
        pack_kernel,
        name="pack",
        grid=(docs // step,),
        out_shape=[shape(docs, width + cols, bf16), shape(8, docs)],
        in_specs=[
            pl.BlockSpec((step, width), lambda i: (i, 0)),
            pl.BlockSpec((step, cols), lambda i: (i, 0)),
        ],
        out_specs=[
            pl.BlockSpec((step, width + cols), lambda i: (i, 0)),
            pl.BlockSpec((8, step), lambda i: (0, i)),
        ],
        cost_estimate=pl.CostEstimate(flops=0, bytes_accessed=4 << 20, transcendentals=0),
    )(documents, labels)
    other_pack = shift_by(pack, "doc", 1)
    top_points = shift_by(skeleton, "doc", -16)
    mid_points = shift_by(skeleton, "doc", 4)

    points, prow, leaf, across, lifted = placed_call(
        functools.partial(leaf_kernel, blocks),
        "leaf",
        [
            shape(rank + tall // blocks, width, bf16),
            shape(8, rank),
            shape(docs, rank, bf16),
            shape(tall, docs, bf16),
            shape(kept, rank),
        ],
        (skeleton, pack, row, transfer),
        [full(skeleton), full(pack), full(row), move(0)],
        flops=2 * docs * rank * width,
    )
    other_points = shift_by(points, "doc", -1)
    lifted = lifted + partner(lifted, "doc", 0)
    sent_mid, lifted = placed_call(
        lift_kernel,
        "lift",
        [shape(tall, rank, bf16), shape(kept, rank)],
        (lifted, partner(lifted, "doc", 1), transfer),
        [full(lifted), full(lifted), move(1)],
    )
    own = call(own_kernel, "own", [shape(kept, docs)], (pack, row, across), flops=2 * docs * docs * width)[0]
    lifted = lifted + partner(lifted, "doc", 2)
    (sent_top,) = call(
        top_kernel, "top", [shape(tall, rank, bf16)], (lifted, partner(lifted, "doc", 3))
    )
    (mid_gram,) = call(gram_kernel, "mid_gram", [shape(rank, rank, bf16)], (points, prow, mid_points))
    (top_gram,) = call(gram_kernel, "top_gram", [shape(rank, rank, bf16)], (points, prow, top_points))
    top_back = shift_by(top_gram, "doc", 16)
    mid_mine, mid_give = call(
        couple_kernel,
        "mid_couple",
        [shape(kept, rank), shape(kept, rank)],
        (mid_gram, sent_mid, shift_by(sent_mid, "doc", 4)),
    )
    low_mine, low_give = call(
        functools.partial(leaf_couple_kernel, blocks),
        "low_couple",
        [shape(kept, rank), shape(kept, rank)],
        (points, prow, other_points),
    )
    mid_back = shift_by(mid_give, "doc", -4)
    low_back = shift_by(low_give, "doc", 1)
    top_before, top_after = swap(sent_top, "doc", 16)
    pair_mine, pair_give = call(
        pair_kernel,
        "pair",
        [shape(kept, docs), shape(kept, docs)],
        (pack, row, across, other_pack),
        flops=2 * docs * docs * width,
    )
    pair_back = shift_by(pair_give, "doc", -1)
    smem = pl.BlockSpec(memory_space=SMEM)
    part = placed_call(
        functools.partial(far_kernel, size),
        "far",
        shape(kept, docs),
        (
            near_peer,
            near_live,
            couple_peer,
            couple_live,
            transfer,
            transfer,
            top_gram,
            top_back,
            top_before,
            top_after,
            mid_mine,
            mid_back,
            low_mine,
            low_back,
            leaf,
            own,
            pair_mine,
        ),
        [smem, smem, smem, smem, move(0), move(1)]
        + [full(v) for v in (top_gram, top_back, top_before, top_after)]
        + [full(mid_mine)] * 4
        + [full(leaf), full(own), full(pair_mine)],
    )
    return placed_call(
        functools.partial(score_kernel, size),
        "score",
        shape(docs, cols),
        (near_peer, near_live, part, pair_back),
        [smem, smem, full(part), full(pair_back)],
    )


def solution(mesh):
    placed = (
        P("doc", None),
        P("doc", None),
        P("doc", None),
        P(),
        P("doc", None),
        P("doc", None),
        P("doc", None, None),
        P("doc", None, None),
    )
    return jax.shard_map(
        local, mesh=mesh, in_specs=placed, out_specs=P("doc", None), check_vma=False
    )
```

```python
import functools
import math

import jax
import jax.numpy as jnp
from jax import lax
from jax.experimental import pallas as pl
from jax.experimental.pallas import tpu as pltpu
from jax.sharding import PartitionSpec as P

f32 = jnp.float32
bf16 = jnp.bfloat16
eps_value = 1e-06
far_gain = 64.0
NN = (((1,), (0,)), ((), ()))
NT = (((1,), (1,)), ((), ()))
VMEM = pltpu.VMEM
SMEM = pltpu.SMEM
step = 256
params = pltpu.CompilerParams(vmem_limit_bytes=24 << 20)


def shift_by(value, axis, by):
    devices = lax.axis_size(axis)
    pairs = [(i, i + by) for i in range(devices) if 0 <= i + by < devices]
    return lax.ppermute(value, axis, pairs)


def partner(block, axis, bit):
    count = lax.axis_size(axis)
    route = []
    for low in range(count):
        high = low | 1 << bit
        if high != low and high < count:
            route += [(low, high), (high, low)]
    return lax.ppermute(block, axis, route)


def swap(value, axis, by):
    count = lax.axis_size(axis)
    if count <= 2 * by:
        pairs = []
        for i in range(count - by):
            pairs += [(i, i + by), (i + by, i)]
        both = lax.ppermute(value, axis, pairs)
        return both, both
    return shift_by(value, axis, by), shift_by(value, axis, -by)


def dot(left, right, dims):
    return lax.dot_general(left, right, dims, preferred_element_type=f32)


def halves(value):
    high = value.astype(bf16)
    return high, (value - high.astype(f32)).astype(bf16)


def dot_wide(left, right, dims):
    left_high, left_low = halves(left)
    right_high, right_low = halves(right)
    return dot(left_high, right_high, dims) + (
        dot(left_high, right_low, dims) + dot(left_low, right_high, dims)
    )


def normalized(rows):
    wide = rows.astype(f32)
    inv_scale = lax.rsqrt(jnp.mean(wide * wide, axis=-1, keepdims=True) + eps_value)
    return (wide * inv_scale).astype(bf16)


def offsets(rows):
    width = rows.shape[1]
    wide = rows.astype(f32)
    total = jnp.sum(wide * wide, axis=1, keepdims=True)
    return (width - total) * (math.log2(math.e) / (2.0 * math.sqrt(width)))


def as_row(column):
    return jnp.transpose(jnp.broadcast_to(column, (column.shape[0], 128)))[0:8]


def as_column(row):
    return jnp.transpose(jnp.broadcast_to(row[0:1], (128, row.shape[1])))[:, 0:1]


def tile(left, left_column, right, right_row):
    width = left.shape[1]
    cross = dot(left, right, NT)
    return jnp.exp2(cross * (math.log2(math.e) / math.sqrt(width)) + (left_column + right_row[0:1]))


def labels_across(labels):
    cols = labels.shape[1]
    across = jnp.transpose(labels.astype(f32))
    ones = (lax.broadcasted_iota(jnp.int32, (16, labels.shape[0]), 0) == 0).astype(f32)
    return jnp.concatenate([across, ones], axis=0).astype(bf16)


def count(peer_ref, live_ref, at, code):
    total = jnp.int32(0)
    for slot in range(peer_ref.shape[-1]):
        where = at + (slot,)
        total = total + live_ref[where] * (peer_ref[where] == code).astype(jnp.int32)
    return total


def tally(peer_ref, live_ref, at, code, exists):
    return (count(peer_ref, live_ref, at, code) * exists.astype(jnp.int32)).astype(f32)


def pack_kernel(docs_ref, labels_ref, pack_ref, row_ref):
    width = docs_ref.shape[1]
    rows = normalized(docs_ref[...])
    pack_ref[:, :width] = rows
    pack_ref[:, width:] = labels_ref[...]
    row_ref[...] = as_row(offsets(rows))


def leaf_kernel(blocks, place_ref, skeleton_ref, pack_ref, row_ref, move_ref, points_ref, prow_ref, leaf_ref, across_ref, lifted_ref, lifted_sent_ref):
    rank, width = skeleton_ref.shape
    docs = pack_ref.shape[0]
    points = normalized(skeleton_ref[...])
    points_ref[0:rank] = points
    prow = as_row(offsets(points))
    prow_ref[...] = prow
    across = labels_across(pack_ref[:, width:])
    across_ref[...] = across
    leaf = tile(pack_ref[:, :width], as_column(row_ref[...]), points, prow).astype(bf16)
    leaf_ref[...] = leaf
    node = dot(across, leaf, NN) * (1.0 / docs)
    sent = node.astype(bf16)
    tall = sent.shape[0] // blocks
    for q in range(blocks):
        points_ref[rank : rank + tall, q * rank : (q + 1) * rank] = sent[q * tall : (q + 1) * tall]
    if blocks * rank < width:
        points_ref[rank : rank + tall, blocks * rank :] = jnp.zeros((tall, width - blocks * rank), bf16)
    lifted = 0.25 * dot_wide(node, move_ref[0, 0], NN)
    lifted_ref[...] = lifted
    lifted_sent_ref[...] = lifted.astype(bf16)


def own_kernel(pack_ref, row_ref, across_ref, out_ref):
    docs = pack_ref.shape[0]
    width = pack_ref.shape[1] - across_ref.shape[0] + 16
    kept = out_ref.shape[0]
    column = as_column(row_ref[...])
    for start in range(0, docs, step):
        part = slice(start, start + step)
        some = tile(pack_ref[:, :width], column, pack_ref[part, :width], row_ref[:, part])
        diagonal = (
            lax.broadcasted_iota(jnp.int32, some.shape, 1) + start
            == lax.broadcasted_iota(jnp.int32, some.shape, 0)
        )
        some = jnp.where(diagonal, 0.0, some).astype(bf16)
        out_ref[:, part] = dot(across_ref[...], some, NN)[0:kept]


def pair_kernel(pack_ref, row_ref, across_ref, other_ref, mine_ref, give_ref):
    docs = pack_ref.shape[0]
    width = pack_ref.shape[1] - across_ref.shape[0] + 16
    kept = mine_ref.shape[0]
    column = as_column(row_ref[...])
    total = jnp.zeros((across_ref.shape[0], docs), f32)
    for start in range(0, docs, step):
        part = slice(start, start + step)
        other = other_ref[part, :width]
        some = tile(pack_ref[:, :width], column, other, as_row(offsets(other))).astype(bf16)
        give_ref[:, part] = dot(across_ref[...], some, NN).astype(bf16)
        total = total + dot(labels_across(other_ref[part, width:]), some, NT)
    mine_ref[...] = total[0:kept]


def gram_kernel(points_ref, prow_ref, other_ref, out_ref):
    rank = other_ref.shape[0]
    other = normalized(other_ref[...])
    out_ref[...] = tile(
        points_ref[0:rank], as_column(prow_ref[...]), other, as_row(offsets(other))
    ).astype(bf16)


def unpack_sent(points_ref, rank, blocks):
    return jnp.concatenate(
        [points_ref[rank:, q * rank : (q + 1) * rank] for q in range(blocks)], axis=0
    )


def leaf_couple_kernel(blocks, points_ref, prow_ref, other_ref, mine_ref, give_ref):
    rank = prow_ref.shape[1]
    kept = mine_ref.shape[0]
    other = other_ref[0:rank]
    gram = tile(
        points_ref[0:rank], as_column(prow_ref[...]), other, as_row(offsets(other))
    ).astype(bf16)
    mine_ref[...] = dot(unpack_sent(other_ref, rank, blocks), gram, NT)[0:kept]
    give_ref[...] = dot(unpack_sent(points_ref, rank, blocks), gram, NN).astype(bf16)


def couple_kernel(gram_ref, sent_ref, other_ref, mine_ref, give_ref):
    kept = mine_ref.shape[0]
    gram = gram_ref[...]
    mine_ref[...] = dot(other_ref[...], gram, NT)[0:kept]
    give_ref[...] = dot(sent_ref[...], gram, NN).astype(bf16)


def lift_kernel(place_ref, mine_ref, other_ref, move_ref, sent_ref, lifted_ref, lifted_sent_ref):
    node = mine_ref[...] + other_ref[...].astype(f32)
    sent_ref[...] = node.astype(bf16)
    lifted = 0.25 * dot_wide(node, move_ref[0, 0], NN)
    lifted_ref[...] = lifted
    lifted_sent_ref[...] = lifted.astype(bf16)


def add_kernel(mine_ref, other_ref, sum_ref, sent_ref):
    total = mine_ref[...] + other_ref[...].astype(f32)
    sum_ref[...] = total
    sent_ref[...] = total.astype(bf16)


def top_kernel(mine_ref, other_ref, sent_ref):
    sent_ref[...] = (mine_ref[...] + other_ref[...].astype(f32)).astype(bf16)


def far_kernel(
    size,
    place_ref,
    near_peer_ref,
    near_live_ref,
    peer_ref,
    live_ref,
    move_low_ref,
    move_high_ref,
    gram_ref,
    back_ref,
    top_before_ref,
    top_after_ref,
    mid_mine_ref,
    mid_give_ref,
    low_mine_ref,
    low_give_ref,
    leaf_ref,
    own_ref,
    pair_ref,
    out_ref,
):
    me = place_ref[0]
    rank = gram_ref.shape[0]
    kept = mid_mine_ref.shape[0]

    def sides(level):
        stride = 4**level
        before = tally(peer_ref, live_ref, (0, level), 0, me >= stride)
        after = tally(peer_ref, live_ref, (0, level), 1, me <= size - 1 - stride)
        return before, after

    scale = 1.0 / rank
    before, after = sides(2)
    down = (
        after * dot(top_after_ref[...], gram_ref[...], NT)
        + before * dot(top_before_ref[...], back_ref[...], NN)
    )[0:kept] * scale
    before, after = sides(1)
    far = (before * mid_mine_ref[...] + after * mid_give_ref[0:kept].astype(f32)) * scale
    down = far + dot_wide(down, move_high_ref[0, 0], NT)
    before, after = sides(0)
    far = (after * low_mine_ref[...] + before * low_give_ref[0:kept].astype(f32)) * scale
    down = far + dot_wide(down, move_low_ref[0, 0], NT)
    high, low = halves(down)
    leaf = leaf_ref[...]
    far = (far_gain / rank) * (dot(high, leaf, NT) + dot(low, leaf, NT))
    before = tally(near_peer_ref, near_live_ref, (0,), 0, me >= 1)
    out_ref[...] = own_ref[...] + before * pair_ref[...] + far


def score_kernel(size, place_ref, near_peer_ref, near_live_ref, part_ref, give_ref, out_ref):
    cols = out_ref.shape[1]
    after = tally(near_peer_ref, near_live_ref, (0,), 1, place_ref[0] <= size - 2)
    total = part_ref[...] + after * give_ref[0 : part_ref.shape[0]].astype(f32)
    out_ref[...] = jnp.transpose(total[0:cols] / total[cols : cols + 1])


def vmem(count):
    return [pl.BlockSpec(memory_space=VMEM)] * count


def call(body, name, outs, ins, flops=0):
    moved = sum(math.prod(o.shape) * o.dtype.itemsize for o in outs)
    moved += sum(math.prod(i.shape) * i.dtype.itemsize for i in ins)
    return pl.pallas_call(
        body,
        name=name,
        compiler_params=params,
        out_shape=outs,
        in_specs=vmem(len(ins)),
        out_specs=vmem(len(outs)),
        cost_estimate=pl.CostEstimate(flops=flops, bytes_accessed=moved, transcendentals=0),
    )(*ins)


def shape(rows, cols, dtype=f32):
    return jax.ShapeDtypeStruct((rows, cols), dtype)


def local(documents, labels, skeleton, transfer, near_peer, near_live, couple_peer, couple_live):
    size = lax.axis_size("doc")
    place = jnp.reshape(lax.axis_index("doc"), (1,)).astype(jnp.int32)
    docs, width = documents.shape
    cols = labels.shape[1]
    rank = skeleton.shape[0]
    kept = cols + 8
    tall = cols + 16
    blocks = max(b for b in range(1, width // rank + 1) if tall % (16 * b) == 0)

    def full(value):
        return pl.BlockSpec(value.shape, lambda i, p: (0,) * value.ndim)

    def move(level):
        return pl.BlockSpec((1, 1, rank, rank), lambda i, p: (level, (p[0] >> (2 * level)) & 3, 0, 0))

    def placed_call(body, name, outs, ins, specs, flops=0):
        return pl.pallas_call(
            body,
            name=name,
            compiler_params=params,
            out_shape=outs,
            grid_spec=pltpu.PrefetchScalarGridSpec(
                num_scalar_prefetch=1,
                grid=(1,),
                in_specs=specs,
                out_specs=[full(o) for o in outs] if isinstance(outs, list) else full(outs),
            ),
            cost_estimate=pl.CostEstimate(flops=flops, bytes_accessed=4 << 20, transcendentals=0),
        )(place, *ins)

    pack, row = pl.pallas_call(
        pack_kernel,
        name="pack",
        compiler_params=params,
        grid=(docs // step,),
        out_shape=[shape(docs, width + cols, bf16), shape(8, docs)],
        in_specs=[
            pl.BlockSpec((step, width), lambda i: (i, 0)),
            pl.BlockSpec((step, cols), lambda i: (i, 0)),
        ],
        out_specs=[
            pl.BlockSpec((step, width + cols), lambda i: (i, 0)),
            pl.BlockSpec((8, step), lambda i: (0, i)),
        ],
        cost_estimate=pl.CostEstimate(flops=0, bytes_accessed=4 << 20, transcendentals=0),
    )(documents, labels)
    other_pack = shift_by(pack, "doc", 1)
    top_points = shift_by(skeleton, "doc", -16)
    mid_points = shift_by(skeleton, "doc", 4)

    points, prow, leaf, across, lifted, lifted_sent = placed_call(
        functools.partial(leaf_kernel, blocks),
        "leaf",
        [
            shape(rank + tall // blocks, width, bf16),
            shape(8, rank),
            shape(docs, rank, bf16),
            shape(tall, docs, bf16),
            shape(tall, rank),
            shape(tall, rank, bf16),
        ],
        (skeleton, pack, row, transfer),
        [full(skeleton), full(pack), full(row), move(0)],
        flops=2 * docs * rank * width,
    )
    other_points = shift_by(points, "doc", -1)
    sums = [shape(tall, rank), shape(tall, rank, bf16)]
    lifted, lifted_sent = call(add_kernel, "add_0", sums, (lifted, partner(lifted_sent, "doc", 0)))
    sent_mid, lifted, lifted_sent = placed_call(
        lift_kernel,
        "lift",
        [shape(tall, rank, bf16)] + sums,
        (lifted, partner(lifted_sent, "doc", 1), transfer),
        [full(lifted), full(lifted), move(1)],
    )
    own = call(own_kernel, "own", [shape(kept, docs)], (pack, row, across), flops=2 * docs * docs * width)[0]
    lifted, lifted_sent = call(add_kernel, "add_2", sums, (lifted, partner(lifted_sent, "doc", 2)))
    (sent_top,) = call(
        top_kernel, "top", [shape(tall, rank, bf16)], (lifted, partner(lifted_sent, "doc", 3))
    )
    (mid_gram,) = call(gram_kernel, "mid_gram", [shape(rank, rank, bf16)], (points, prow, mid_points))
    (top_gram,) = call(gram_kernel, "top_gram", [shape(rank, rank, bf16)], (points, prow, top_points))
    top_back = shift_by(top_gram, "doc", 16)
    mid_mine, mid_give = call(
        couple_kernel,
        "mid_couple",
        [shape(kept, rank), shape(tall, rank, bf16)],
        (mid_gram, sent_mid, shift_by(sent_mid, "doc", 4)),
    )
    low_mine, low_give = call(
        functools.partial(leaf_couple_kernel, blocks),
        "low_couple",
        [shape(kept, rank), shape(tall, rank, bf16)],
        (points, prow, other_points),
    )
    mid_back = shift_by(mid_give, "doc", -4)
    low_back = shift_by(low_give, "doc", 1)
    top_before, top_after = swap(sent_top, "doc", 16)
    pair_mine, pair_give = call(
        pair_kernel,
        "pair",
        [shape(kept, docs), shape(tall, docs, bf16)],
        (pack, row, across, other_pack),
        flops=2 * docs * docs * width,
    )
    pair_back = shift_by(pair_give, "doc", -1)
    smem = pl.BlockSpec(memory_space=SMEM)
    part = placed_call(
        functools.partial(far_kernel, size),
        "far",
        shape(kept, docs),
        (
            near_peer,
            near_live,
            couple_peer,
            couple_live,
            transfer,
            transfer,
            top_gram,
            top_back,
            top_before,
            top_after,
            mid_mine,
            mid_back,
            low_mine,
            low_back,
            leaf,
            own,
            pair_mine,
        ),
        [smem, smem, smem, smem, move(0), move(1)]
        + [full(v) for v in (top_gram, top_back, top_before, top_after)]
        + [full(v) for v in (mid_mine, mid_back, low_mine, low_back)]
        + [full(leaf), full(own), full(pair_mine)],
    )
    return placed_call(
        functools.partial(score_kernel, size),
        "score",
        shape(docs, cols),
        (near_peer, near_live, part, pair_back),
        [smem, smem, full(part), full(pair_back)],
    )


def solution(mesh):
    placed = (
        P("doc", None),
        P("doc", None),
        P("doc", None),
        P(),
        P("doc", None),
        P("doc", None),
        P("doc", None, None),
        P("doc", None, None),
    )
    return jax.shard_map(
        local, mesh=mesh, in_specs=placed, out_specs=P("doc", None), check_vma=False
    )
```

```python
import functools
import math

import jax
import jax.numpy as jnp
from jax import lax
from jax.experimental import pallas as pl
from jax.experimental.pallas import tpu as pltpu
from jax.sharding import PartitionSpec as P


f32 = jnp.float32
bf16 = jnp.bfloat16
eps_value = 1e-06
far_gain = 64.0
NN = (((1,), (0,)), ((), ()))
NT = (((1,), (1,)), ((), ()))
VMEM = pltpu.VMEM
SMEM = pltpu.SMEM
step = 256
params = pltpu.CompilerParams(vmem_limit_bytes=24 << 20)


def routed(value, pairs):
    return lax.ppermute(value, "doc", pairs)


def shift_by(value, by):
    count = lax.axis_size("doc")
    return routed(value, [(i, i + by) for i in range(count) if 0 <= i + by < count])


def partner(value, bit, every=1):
    count = lax.axis_size("doc")
    route = []
    for low in range(0, count, every):
        high = low | 1 << bit
        if high != low and high < count:
            route += [(low, high), (high, low)]
    return routed(value, route)


def swap(value, by):
    count = lax.axis_size("doc")
    if count <= 2 * by:
        pairs = []
        for i in range(count - by):
            pairs += [(i, i + by), (i + by, i)]
        both = routed(value, pairs)
        return both, both
    return shift_by(value, by), shift_by(value, -by)


def swap_cross(value, by, bit):
    count = lax.axis_size("doc")
    flip = 1 << bit

    def pairs(shift):
        ends = [(i ^ flip, i + shift) for i in range(count) if 0 <= i + shift < count]
        return [(low, high) for low, high in ends if low < count]

    if count <= 2 * by:
        both = routed(value, pairs(by) + pairs(-by))
        return both, both
    return routed(value, pairs(by)), routed(value, pairs(-by))


def goes_down(place):
    return (place % 2 == 0) | ((place // 2) % 4 == 3)


def top_routes(count):
    pairs = []
    for i in range(count - 16):
        pairs.append((i + 16, i) if goes_down(i) else (i, i + 16))
    return pairs


def slots_first(lists):
    return jnp.transpose(lists, (0, 2, 1))[0]


def in_hbm(value):
    return pltpu.with_memory_space_constraint(value, pltpu.HBM)


def dot(left, right, dims):
    return lax.dot_general(left, right, dims, preferred_element_type=f32)


def halves(value):
    high = value.astype(bf16)
    return high, (value - high.astype(f32)).astype(bf16)


def dot_wide(left, right, dims):
    left_high, left_low = halves(left)
    right_high, right_low = halves(right)
    return dot(left_high, right_high, dims) + (
        dot(left_high, right_low, dims) + dot(left_low, right_high, dims)
    )


def normalized(rows):
    wide = rows.astype(f32)
    inv_scale = lax.rsqrt(jnp.mean(wide * wide, axis=-1, keepdims=True) + eps_value)
    return (wide * inv_scale).astype(bf16)


def offsets(rows):
    width = rows.shape[1]
    wide = rows.astype(f32)
    total = jnp.sum(wide * wide, axis=1, keepdims=True)
    return (width - total) * (math.log2(math.e) / (2.0 * math.sqrt(width)))


def as_row(column):
    return jnp.transpose(jnp.broadcast_to(column, (column.shape[0], 128)))[0:8]


def as_column(row):
    return jnp.transpose(jnp.broadcast_to(row[0:1], (128, row.shape[1])))[:, 0:1]


def tile(left, left_column, right, right_row):
    width = left.shape[1]
    cross = dot(left, right, NT)
    return jnp.exp2(cross * (math.log2(math.e) / math.sqrt(width)) + (left_column + right_row[0:1]))


def labels_across(labels):
    across = jnp.transpose(labels.astype(f32))
    ones = (lax.broadcasted_iota(jnp.int32, (16, labels.shape[0]), 0) == 0).astype(f32)
    return jnp.concatenate([across, ones], axis=0).astype(bf16)


def tallies(size, me, near_peer_ref, near_live_ref, peer_ref, live_ref, counts_ref):
    sides = counts_ref.shape[0] // 2
    slots = near_peer_ref.shape[1]
    for place in range(sides):
        stride = 4 ** max(place - 1, 0)
        for code, exists in ((0, me >= stride), (1, me <= size - 1 - stride)):
            total = jnp.int32(0)
            for slot in range(slots):
                if place == 0:
                    peer, live = near_peer_ref[0, slot], near_live_ref[0, slot]
                else:
                    peer, live = peer_ref[slot, place - 1], live_ref[slot, place - 1]
                total = total + live * (peer == code).astype(jnp.int32)
            counts_ref[code * sides + place] = (total * exists.astype(jnp.int32)).astype(f32)


def leaf_kernel(
    size,
    place_ref,
    near_peer_hbm,
    near_live_hbm,
    peer_hbm,
    live_hbm,
    moves_ref,
    docs_ref,
    skeleton_hbm,
    labels_hbm,
    counts_ref,
    rows_ref,
    row_ref,
    points_ref,
    prow_ref,
    leaf_ref,
    across_ref,
    lifted_ref,
    lifted_sent_ref,
    low_move_ref,
    high_move_ref,
    first_ref,
    last_ref,
    skeleton_ref,
    labels_ref,
    near_peer_ref,
    near_live_ref,
    peer_ref,
    live_ref,
    sems,
):
    docs, _ = rows_ref.shape
    rank = skeleton_ref.shape[0]
    me = place_ref[0]
    parts = [slice(start, start + step) for start in range(0, docs, step)]
    split = first_ref.shape[0]
    targets = [
        first_ref.at[part] if part.stop <= split else last_ref.at[part.start - split : part.stop - split]
        for part in parts
    ]
    loads = [
        pltpu.make_async_copy(docs_ref.at[part], target, sems.at[2 + i])
        for i, (part, target) in enumerate(zip(parts, targets))
    ]
    low = pltpu.make_async_copy(moves_ref.at[0, me & 3], low_move_ref, sems.at[0])
    high = pltpu.make_async_copy(moves_ref.at[1, (me >> 2) & 3], high_move_ref, sems.at[1])
    ends = 2 + len(parts)
    firsts = [
        pltpu.make_async_copy(source, target, sems.at[ends + i])
        for i, (source, target) in enumerate(
            [
                (skeleton_hbm, skeleton_ref),
                (labels_hbm, labels_ref),
                (near_peer_hbm, near_peer_ref),
                (near_live_hbm, near_live_ref),
                (peer_hbm, peer_ref),
                (live_hbm, live_ref),
            ]
        )
    ]
    for load in firsts + loads + [low, high]:
        load.start()
    firsts[0].wait()
    points = normalized(skeleton_ref[...])
    points_ref[...] = points
    prow = as_row(offsets(points))
    prow_ref[...] = prow
    firsts[1].wait()
    across = labels_across(labels_ref[...])
    across_ref[:, :docs] = across
    node = jnp.zeros((across.shape[0], rank), f32)
    for part, target, load in zip(parts, targets, loads):
        load.wait()
        rows = normalized(target[...])
        rows_ref[part] = rows
        column = offsets(rows)
        row_ref[:, part] = as_row(column)
        leaf = tile(rows, column, points, prow).astype(bf16)
        leaf_ref[part] = leaf
        node = node + dot(across[:, part], leaf, NN)
    node = node * (1.0 / docs)
    across_ref[:, docs:] = node.astype(bf16)
    low.wait()
    lifted = 0.25 * dot_wide(node, low_move_ref[...], NN)
    lifted_ref[...] = lifted
    lifted_sent_ref[...] = lifted.astype(bf16)
    high.wait()
    for load in firsts[2:]:
        load.wait()
    tallies(size, me, near_peer_ref, near_live_ref, peer_ref, live_ref, counts_ref)


def own_kernel(rows_ref, row_ref, across_ref, out_ref):
    docs = rows_ref.shape[0]
    kept = out_ref.shape[0]
    column = as_column(row_ref[...])
    for start in range(0, docs, step):
        part = slice(start, start + step)
        some = tile(rows_ref[...], column, rows_ref[part], row_ref[:, part])
        diagonal = (
            lax.broadcasted_iota(jnp.int32, some.shape, 1) + start
            == lax.broadcasted_iota(jnp.int32, some.shape, 0)
        )
        some = jnp.where(diagonal, 0.0, some).astype(bf16)
        out_ref[:, part] = dot(across_ref[:, :docs], some, NN)[0:kept]


def tile_kernel(rows_ref, row_ref, across_ref, other_ref, *refs):
    docs = rows_ref.shape[0]
    part = other_ref.shape[0]
    tile_ref, back_ref = refs[-2:]
    if len(refs) > 2:
        back_ref[:, part:] = refs[0][...]
    column = as_column(row_ref[...])
    for start in range(0, part, step):
        here = slice(start, start + step)
        other = normalized(other_ref[here])
        some = tile(rows_ref[...], column, other, as_row(offsets(other))).astype(bf16)
        tile_ref[:, here] = some
        back_ref[:, here] = dot(across_ref[:, :docs], some, NN).astype(bf16)


def low_kernel(docs, points_ref, prow_ref, across_ref, other_ref, gram_ref, give_ref):
    other = normalized(other_ref[...])
    gram = tile(points_ref[...], as_column(prow_ref[...]), other, as_row(offsets(other)))
    gram = gram.astype(bf16)
    gram_ref[...] = gram
    give_ref[...] = dot(across_ref[:, docs:], gram, NN).astype(bf16)


def near_kernel(first_ref, last_ref, gram_ref, other_ref, pair_ref, low_ref):
    kept, docs = pair_ref.shape
    split = first_ref.shape[1]
    pair = dot(other_ref[:, :split], first_ref[...], NT)
    pair = pair + dot(other_ref[:, split:docs], last_ref[...], NT)
    pair_ref[...] = pair[0:kept]
    low_ref[...] = dot(other_ref[:, docs:], gram_ref[...], NT)[0:kept]


def gram_kernel(points_ref, prow_ref, other_ref, out_ref):
    other = normalized(other_ref[...])
    out_ref[...] = tile(
        points_ref[...], as_column(prow_ref[...]), other, as_row(offsets(other))
    ).astype(bf16)


def couple_kernel(gram_ref, sent_ref, other_ref, mine_ref, give_ref):
    kept = mine_ref.shape[0]
    gram = gram_ref[...]
    mine_ref[...] = dot(other_ref[...], gram, NT)[0:kept]
    give_ref[...] = dot(sent_ref[...], gram, NN).astype(bf16)


def take_kernel(mine_ref, other_ref, move_ref, sent_ref, lifted_ref, lifted_sent_ref):
    node = mine_ref[...] + other_ref[...].astype(f32)
    sent_ref[...] = node.astype(bf16)
    lifted = 0.25 * dot_wide(node, move_ref[...], NN)
    lifted_ref[...] = lifted
    lifted_sent_ref[...] = lifted.astype(bf16)


def add_kernel(mine_ref, other_ref, sum_ref, sent_ref):
    total = mine_ref[...] + other_ref[...].astype(f32)
    sum_ref[...] = total
    sent_ref[...] = total.astype(bf16)


def top_kernel(mine_ref, other_ref, sent_ref):
    sent_ref[...] = (mine_ref[...] + other_ref[...].astype(f32)).astype(bf16)


def far_kernel(
    paired,
    counts_ref,
    downward_ref,
    move_low_ref,
    move_high_ref,
    gram_ref,
    back_ref,
    before_ref,
    before_cross_ref,
    after_ref,
    after_cross_ref,
    mid_mine_ref,
    mid_give_ref,
    low_mine_ref,
    leaf_ref,
    own_ref,
    pair_ref,
    out_ref,
):
    rank = gram_ref.shape[0]
    kept = mid_mine_ref.shape[0]
    sides = counts_ref.shape[0] // 2

    def before(level):
        return counts_ref[1 + level]

    def after(level):
        return counts_ref[sides + 1 + level]

    def sent(one_ref, two_ref):
        return one_ref[...].astype(f32) + two_ref[...].astype(f32)

    scale = 1.0 / rank
    downward = downward_ref[0] == 1
    came = returned = sent(after_ref, after_cross_ref)
    if not paired:
        other = sent(before_ref, before_cross_ref)
        came = jnp.where(downward, came, other)
        returned = jnp.where(downward, other, returned)
    came_count = jnp.where(downward, after(2), before(2))
    returned_count = jnp.where(downward, before(2), after(2))
    down = came_count * dot(came.astype(bf16), gram_ref[...], NT) + returned_count * dot(
        returned.astype(bf16), back_ref[...], NN
    )
    down = down[0:kept] * scale
    far = (after(1) * mid_mine_ref[...] + before(1) * mid_give_ref[0:kept].astype(f32)) * scale
    down = far + dot_wide(down, move_high_ref[...], NT)
    far = before(0) * low_mine_ref[...] * scale
    down = far + dot_wide(down, move_low_ref[...], NT)
    high, low = halves(down)
    leaf = leaf_ref[...]
    far = (far_gain / rank) * (dot(high, leaf, NT) + dot(low, leaf, NT))
    out_ref[...] = own_ref[...] + counts_ref[0] * pair_ref[...] + far


def score_kernel(counts_ref, part_ref, leaf_ref, first_ref, last_ref, out_ref):
    docs, cols = out_ref.shape
    rank = leaf_ref.shape[1]
    kept = part_ref.shape[0]
    sides = counts_ref.shape[0] // 2
    split = first_ref.shape[1] - rank
    far = (counts_ref[sides + 1] * (far_gain / rank / rank)) * dot(first_ref[:, split:], leaf_ref[...], NT)
    total = part_ref[...] + far[0:kept]

    def finish(part, given):
        some = total[:, part] + counts_ref[sides] * given[0:kept].astype(f32)
        out_ref[part] = jnp.transpose(some[0:cols] / some[cols : cols + 1])

    finish(slice(0, split), first_ref[:, :split])
    finish(slice(split, docs), last_ref[...])


def vmem(count):
    return [pl.BlockSpec(memory_space=VMEM)] * count


def call(body, outs, ins, flops=0, scalars=()):
    moved = sum(math.prod(o.shape) * o.dtype.itemsize for o in outs)
    moved += sum(math.prod(i.shape) * i.dtype.itemsize for i in ins)
    return pl.pallas_call(
        body,
        compiler_params=params,
        out_shape=outs,
        in_specs=[pl.BlockSpec(memory_space=SMEM)] * len(scalars) + vmem(len(ins)),
        out_specs=vmem(len(outs)),
        cost_estimate=pl.CostEstimate(flops=flops, bytes_accessed=moved, transcendentals=0),
    )(*scalars, *ins)


def shape(rows, cols, dtype=f32):
    return jax.ShapeDtypeStruct((rows, cols), dtype)


def local(documents, labels, skeleton, transfer, near_peer, near_live, couple_peer, couple_live):
    size = lax.axis_size("doc")
    place = jnp.reshape(lax.axis_index("doc"), (1,)).astype(jnp.int32)
    docs, width = documents.shape
    cols = labels.shape[1]
    rank = skeleton.shape[0]
    kept = cols + 8
    tall = cols + 16

    sums = [shape(tall, rank), shape(tall, rank, bf16)]
    products = [shape(kept, rank), shape(tall, rank, bf16)]
    square = shape(rank, rank)
    split = docs - step
    smem = pl.BlockSpec(memory_space=SMEM)
    hbm = pl.BlockSpec(memory_space=pltpu.HBM)

    mid_points = shift_by(skeleton, -4)
    outs = pl.pallas_call(
        functools.partial(leaf_kernel, size),
        name="leaf",
        compiler_params=params,
        out_shape=[
            jax.ShapeDtypeStruct((2 * (1 + couple_peer.shape[1]),), f32),
            shape(docs, width, bf16),
            shape(8, docs),
            shape(rank, width, bf16),
            shape(8, rank),
            shape(docs, rank, bf16),
            shape(tall, docs + rank, bf16),
        ]
        + sums
        + [square, square, shape(split, width, bf16), shape(docs - split, width, bf16)],
        in_specs=[smem] + [hbm] * 8,
        out_specs=[smem] + vmem(12),
        scratch_shapes=[
            VMEM((rank, width), bf16),
            VMEM((docs, cols), bf16),
            SMEM(near_peer.shape, jnp.int32),
            SMEM(near_peer.shape, jnp.int32),
            SMEM(couple_peer.shape[:0:-1], jnp.int32),
            SMEM(couple_peer.shape[:0:-1], jnp.int32),
            pltpu.SemaphoreType.DMA((8 + docs // step,)),
        ],
        cost_estimate=pl.CostEstimate(
            flops=2 * docs * rank * width, bytes_accessed=4 << 20, transcendentals=0
        ),
    )(place, in_hbm(near_peer), in_hbm(near_live), in_hbm(slots_first(couple_peer)), in_hbm(slots_first(couple_live)), in_hbm(transfer), in_hbm(documents), in_hbm(skeleton), in_hbm(labels))
    counts, rows, row, points, prow, leaf, across, lifted, lifted_sent = outs[:9]
    low_move, high_move, first_docs, last_docs = outs[9:]
    lifted, lifted_sent = call(add_kernel, sums, (lifted, partner(lifted_sent, 0)))
    sent_mid, lifted, lifted_sent = call(
        take_kernel, [shape(tall, rank, bf16)] + sums, (lifted, partner(lifted_sent, 1), high_move)
    )
    other_low = shift_by(skeleton, 1)
    first_docs = shift_by(first_docs, 1)
    last_docs = shift_by(last_docs, 1)
    other_labels = shift_by(across, 1)
    top_points = routed(skeleton, top_routes(size))
    (own,) = call(
        own_kernel, [shape(kept, docs)], (rows, row, across), flops=2 * docs * docs * width
    )
    (top,) = call(top_kernel, [shape(tall, rank, bf16)], (lifted, partner(lifted_sent, 2)))
    top_before, top_after = swap(top, 16)
    paired = top_before is top_after
    cross_before, cross_after = swap_cross(top, 16, 3)
    other_mid = shift_by(sent_mid, -4)
    gram = [shape(rank, rank, bf16)]
    low_gram, low_give = call(
        functools.partial(low_kernel, docs),
        gram + [shape(tall, rank, bf16)],
        (points, prow, across, other_low),
    )
    (mid_gram,) = call(gram_kernel, gram, (points, prow, mid_points))
    (top_gram,) = call(gram_kernel, gram, (points, prow, top_points))
    top_back = routed(top_gram, [(j, i) for i, j in top_routes(size)])
    mid_mine, mid_give = call(couple_kernel, products, (mid_gram, sent_mid, other_mid))
    mid_back = shift_by(mid_give, 4)
    shared = (rows, row, across)
    first_tile, first_back = call(
        tile_kernel,
        [shape(docs, split, bf16), shape(tall, split + rank, bf16)],
        (*shared, first_docs, low_give),
        flops=2 * docs * split * width,
    )
    last_tile, last_back = call(
        tile_kernel,
        [shape(docs, docs - split, bf16), shape(tall, docs - split, bf16)],
        (*shared, last_docs),
        flops=2 * docs * (docs - split) * width,
    )
    first_back = shift_by(first_back, -1)
    last_back = shift_by(last_back, -1)
    pair_mine, low_mine = call(
        near_kernel,
        [shape(kept, docs), shape(kept, rank)],
        (first_tile, last_tile, low_gram, other_labels),
    )
    (part,) = call(
        functools.partial(far_kernel, paired),
        [shape(kept, docs)],
        (
            low_move,
            high_move,
            top_gram,
            top_back,
            top_before,
            cross_before,
            top_after,
            cross_after,
            mid_mine,
            mid_back,
            low_mine,
            leaf,
            own,
            pair_mine,
        ),
        scalars=(counts, goes_down(place).astype(jnp.int32)),
    )
    return call(
        score_kernel, [shape(docs, cols)], (part, leaf, first_back, last_back), scalars=(counts,)
    )[0]


def solution(mesh):
    placed = (
        P("doc", None),
        P("doc", None),
        P("doc", None),
        P(),
        P("doc", None),
        P("doc", None),
        P("doc", None, None),
        P("doc", None, None),
    )
    return jax.shard_map(
        local, mesh=mesh, in_specs=placed, out_specs=P("doc", None), check_vma=False
    )
```

```python
import functools
import math

import jax
import jax.numpy as jnp
from jax import lax
from jax.experimental import pallas as pl
from jax.experimental.pallas import tpu as pltpu
from jax.sharding import PartitionSpec as P


f32 = jnp.float32
bf16 = jnp.bfloat16
eps_value = 1e-06
far_gain = 64.0
NN = (((1,), (0,)), ((), ()))
NT = (((1,), (1,)), ((), ()))
VMEM = pltpu.VMEM
SMEM = pltpu.SMEM
step = 256
params = pltpu.CompilerParams(vmem_limit_bytes=24 << 20)


def routed(value, pairs):
    return lax.ppermute(value, "doc", pairs)


def shift_by(value, by):
    count = lax.axis_size("doc")
    return routed(value, [(i, i + by) for i in range(count) if 0 <= i + by < count])


def partner(value, bit, every=1):
    count = lax.axis_size("doc")
    route = []
    for low in range(0, count, every):
        high = low | 1 << bit
        if high != low and high < count:
            route += [(low, high), (high, low)]
    return routed(value, route)


def swap(value, by):
    count = lax.axis_size("doc")
    if count <= 2 * by:
        pairs = []
        for i in range(count - by):
            pairs += [(i, i + by), (i + by, i)]
        both = routed(value, pairs)
        return both, both
    return shift_by(value, by), shift_by(value, -by)


def swap_cross(value, by, bit):
    count = lax.axis_size("doc")
    flip = 1 << bit

    def pairs(shift):
        ends = [(i ^ flip, i + shift) for i in range(count) if 0 <= i + shift < count]
        return [(low, high) for low, high in ends if low < count]

    if count <= 2 * by:
        both = routed(value, pairs(by) + pairs(-by))
        return both, both
    return routed(value, pairs(by)), routed(value, pairs(-by))


def goes_down(place):
    return place % 2 == 0


def top_routes(count):
    pairs = []
    for i in range(count - 16):
        pairs.append((i + 16, i) if goes_down(i) else (i, i + 16))
    return pairs


def slots_first(lists):
    return jnp.transpose(lists, (0, 2, 1))[0]


def in_hbm(value):
    return pltpu.with_memory_space_constraint(value, pltpu.HBM)


def dot(left, right, dims):
    return lax.dot_general(left, right, dims, preferred_element_type=f32)


def halves(value):
    high = value.astype(bf16)
    return high, (value - high.astype(f32)).astype(bf16)


def dot_wide(left, right, dims):
    left_high, left_low = halves(left)
    right_high, right_low = halves(right)
    return dot(left_high, right_high, dims) + (
        dot(left_high, right_low, dims) + dot(left_low, right_high, dims)
    )


def normalized(rows):
    wide = rows.astype(f32)
    inv_scale = lax.rsqrt(jnp.mean(wide * wide, axis=-1, keepdims=True) + eps_value)
    return (wide * inv_scale).astype(bf16)


def offsets(rows):
    width = rows.shape[1]
    wide = rows.astype(f32)
    total = jnp.sum(wide * wide, axis=1, keepdims=True)
    return (width - total) * (math.log2(math.e) / (2.0 * math.sqrt(width)))


def as_row(column):
    return jnp.transpose(jnp.broadcast_to(column, (column.shape[0], 128)))[0:8]


def as_column(row):
    return jnp.transpose(jnp.broadcast_to(row[0:1], (128, row.shape[1])))[:, 0:1]


def tile(left, left_column, right, right_row):
    width = left.shape[1]
    cross = dot(left, right, NT)
    return jnp.exp2(cross * (math.log2(math.e) / math.sqrt(width)) + (left_column + right_row[0:1]))


def labels_across(labels):
    across = jnp.transpose(labels.astype(f32))
    ones = (lax.broadcasted_iota(jnp.int32, (16, labels.shape[0]), 0) == 0).astype(f32)
    return jnp.concatenate([across, ones], axis=0).astype(bf16)


def tallies(size, me, near_peer_ref, near_live_ref, peer_ref, live_ref, counts_ref):
    sides = counts_ref.shape[0] // 2
    slots = near_peer_ref.shape[1]
    for place in range(sides):
        stride = 4 ** max(place - 1, 0)
        for code, exists in ((0, me >= stride), (1, me <= size - 1 - stride)):
            total = jnp.int32(0)
            for slot in range(slots):
                if place == 0:
                    peer, live = near_peer_ref[0, slot], near_live_ref[0, slot]
                else:
                    peer, live = peer_ref[slot, place - 1], live_ref[slot, place - 1]
                total = total + live * (peer == code).astype(jnp.int32)
            counts_ref[code * sides + place] = (total * exists.astype(jnp.int32)).astype(f32)


def leaf_kernel(
    size,
    place_ref,
    near_peer_hbm,
    near_live_hbm,
    peer_hbm,
    live_hbm,
    moves_ref,
    docs_ref,
    skeleton_hbm,
    labels_hbm,
    counts_ref,
    rows_ref,
    row_ref,
    points_ref,
    prow_ref,
    leaf_ref,
    across_ref,
    lifted_ref,
    lifted_sent_ref,
    low_move_ref,
    high_move_ref,
    first_ref,
    last_ref,
    skeleton_ref,
    labels_ref,
    near_peer_ref,
    near_live_ref,
    peer_ref,
    live_ref,
    sems,
):
    docs, _ = rows_ref.shape
    rank = skeleton_ref.shape[0]
    me = place_ref[0]
    parts = [slice(start, start + step) for start in range(0, docs, step)]
    split = first_ref.shape[0]
    targets = [
        first_ref.at[part] if part.stop <= split else last_ref.at[part.start - split : part.stop - split]
        for part in parts
    ]
    loads = [
        pltpu.make_async_copy(docs_ref.at[part], target, sems.at[2 + i])
        for i, (part, target) in enumerate(zip(parts, targets))
    ]
    low = pltpu.make_async_copy(moves_ref.at[0, me & 3], low_move_ref, sems.at[0])
    high = pltpu.make_async_copy(moves_ref.at[1, (me >> 2) & 3], high_move_ref, sems.at[1])
    ends = 2 + len(parts)
    firsts = [
        pltpu.make_async_copy(source, target, sems.at[ends + i])
        for i, (source, target) in enumerate(
            [
                (skeleton_hbm, skeleton_ref),
                (labels_hbm, labels_ref),
                (near_peer_hbm, near_peer_ref),
                (near_live_hbm, near_live_ref),
                (peer_hbm, peer_ref),
                (live_hbm, live_ref),
            ]
        )
    ]
    for load in firsts[:1] + loads + firsts[1:] + [low, high]:
        load.start()
    firsts[0].wait()
    points = normalized(skeleton_ref[...])
    points_ref[...] = points
    prow = as_row(offsets(points))
    prow_ref[...] = prow
    firsts[1].wait()
    across = labels_across(labels_ref[...])
    across_ref[:, :docs] = across
    node = jnp.zeros((across.shape[0], rank), f32)
    for part, target, load in zip(parts, targets, loads):
        load.wait()
        rows = normalized(target[...])
        rows_ref[part] = rows
        column = offsets(rows)
        row_ref[:, part] = as_row(column)
        leaf = tile(rows, column, points, prow).astype(bf16)
        leaf_ref[part] = leaf
        node = node + dot(across[:, part], leaf, NN)
    node = node * (1.0 / docs)
    across_ref[:, docs:] = node.astype(bf16)
    low.wait()
    lifted = 0.25 * dot_wide(node, low_move_ref[...], NN)
    lifted_ref[...] = lifted
    lifted_sent_ref[...] = lifted.astype(bf16)
    high.wait()
    for load in firsts[2:]:
        load.wait()
    tallies(size, me, near_peer_ref, near_live_ref, peer_ref, live_ref, counts_ref)


def own_kernel(rows_ref, row_ref, across_ref, out_ref):
    docs = rows_ref.shape[0]
    kept = out_ref.shape[0]
    column = as_column(row_ref[...])
    for start in range(0, docs, step):
        part = slice(start, start + step)
        some = tile(rows_ref[...], column, rows_ref[part], row_ref[:, part])
        diagonal = (
            lax.broadcasted_iota(jnp.int32, some.shape, 1) + start
            == lax.broadcasted_iota(jnp.int32, some.shape, 0)
        )
        some = jnp.where(diagonal, 0.0, some).astype(bf16)
        out_ref[:, part] = dot(across_ref[:, :docs], some, NN)[0:kept]


def tile_kernel(rows_ref, row_ref, across_ref, other_ref, *refs):
    docs = rows_ref.shape[0]
    part = other_ref.shape[0]
    tile_ref, back_ref = refs[-2:]
    if len(refs) > 2:
        back_ref[:, part:] = refs[0][...]
    column = as_column(row_ref[...])
    for start in range(0, part, step):
        here = slice(start, start + step)
        other = normalized(other_ref[here])
        some = tile(rows_ref[...], column, other, as_row(offsets(other))).astype(bf16)
        tile_ref[:, here] = some
        back_ref[:, here] = dot(across_ref[:, :docs], some, NN).astype(bf16)


def low_kernel(docs, points_ref, prow_ref, across_ref, other_ref, gram_ref, give_ref):
    other = normalized(other_ref[...])
    gram = tile(points_ref[...], as_column(prow_ref[...]), other, as_row(offsets(other)))
    gram = gram.astype(bf16)
    gram_ref[...] = gram
    give_ref[...] = dot(across_ref[:, docs:], gram, NN).astype(bf16)


def gram_kernel(points_ref, prow_ref, other_ref, out_ref):
    other = normalized(other_ref[...])
    out_ref[...] = tile(
        points_ref[...], as_column(prow_ref[...]), other, as_row(offsets(other))
    ).astype(bf16)


def couple_kernel(gram_ref, sent_ref, other_ref, mine_ref, give_ref):
    kept = mine_ref.shape[0]
    gram = gram_ref[...]
    mine_ref[...] = dot(other_ref[...], gram, NT)[0:kept]
    give_ref[...] = dot(sent_ref[...], gram, NN).astype(bf16)


def take_kernel(mine_ref, other_ref, move_ref, sent_ref, lifted_ref, lifted_sent_ref):
    node = mine_ref[...] + other_ref[...].astype(f32)
    sent_ref[...] = node.astype(bf16)
    lifted = 0.25 * dot_wide(node, move_ref[...], NN)
    lifted_ref[...] = lifted
    lifted_sent_ref[...] = lifted.astype(bf16)


def add_kernel(mine_ref, other_ref, sum_ref, sent_ref):
    total = mine_ref[...] + other_ref[...].astype(f32)
    sum_ref[...] = total
    sent_ref[...] = total.astype(bf16)


def top_kernel(mine_ref, other_ref, sent_ref):
    sent_ref[...] = (mine_ref[...] + other_ref[...].astype(f32)).astype(bf16)


def far_kernel(
    paired,
    counts_ref,
    downward_ref,
    move_low_ref,
    move_high_ref,
    gram_ref,
    back_ref,
    before_ref,
    before_cross_ref,
    after_ref,
    after_cross_ref,
    mid_mine_ref,
    mid_give_ref,
    leaf_ref,
    own_ref,
    out_ref,
):
    rank = gram_ref.shape[0]
    kept = mid_mine_ref.shape[0]
    sides = counts_ref.shape[0] // 2

    def before(level):
        return counts_ref[1 + level]

    def after(level):
        return counts_ref[sides + 1 + level]

    def sent(one_ref, two_ref):
        return one_ref[...].astype(f32) + two_ref[...].astype(f32)

    scale = 1.0 / rank
    downward = downward_ref[0] == 1
    came = returned = sent(after_ref, after_cross_ref)
    if not paired:
        other = sent(before_ref, before_cross_ref)
        came = jnp.where(downward, came, other)
        returned = jnp.where(downward, other, returned)
    came_count = jnp.where(downward, after(2), before(2))
    returned_count = jnp.where(downward, before(2), after(2))
    down = came_count * dot(came.astype(bf16), gram_ref[...], NT) + returned_count * dot(
        returned.astype(bf16), back_ref[...], NN
    )
    down = down[0:kept] * scale
    far = (after(1) * mid_mine_ref[...] + before(1) * mid_give_ref[0:kept].astype(f32)) * scale
    down = far + dot_wide(down, move_high_ref[...], NT)
    down = dot_wide(down, move_low_ref[...], NT)
    high, low = halves(down)
    leaf = leaf_ref[...]
    far = (far_gain / rank) * (dot(high, leaf, NT) + dot(low, leaf, NT))
    out_ref[...] = own_ref[...] + far


def score_kernel(
    counts_ref,
    part_ref,
    leaf_ref,
    gram_ref,
    other_ref,
    first_tile_ref,
    last_tile_ref,
    first_ref,
    last_ref,
    out_ref,
    rows_ref,
    sems,
):
    docs, cols = out_ref.shape
    rank = leaf_ref.shape[1]
    kept = part_ref.shape[0]
    sides = counts_ref.shape[0] // 2
    split = first_ref.shape[1] - rank
    low = counts_ref[1] * dot(other_ref[:, docs:], gram_ref[...], NT)
    low = low + counts_ref[sides + 1] * first_ref[:, split:].astype(f32)
    high, low = halves(low * (1.0 / rank))
    sends = []
    for start in range(0, docs, step):
        part = slice(start, start + step)
        leaf = leaf_ref[part]
        total = (far_gain / rank) * (dot(high, leaf, NT) + dot(low, leaf, NT))
        pair = dot(other_ref[:, :split], first_tile_ref[part], NT)
        pair = pair + dot(other_ref[:, split:docs], last_tile_ref[part], NT)
        total = total + counts_ref[0] * pair
        given = first_ref[:, part] if start < split else last_ref[:, start - split : start - split + step]
        total = total + counts_ref[sides] * given.astype(f32)
        total = part_ref[:, part] + total[0:kept]
        rows_ref[part] = jnp.transpose(total[0:cols] / total[cols : cols + 1])
        sends.append(pltpu.make_async_copy(rows_ref.at[part], out_ref.at[part], sems.at[start // step]))
        sends[-1].start()
    for send in sends:
        send.wait()


def vmem(count):
    return [pl.BlockSpec(memory_space=VMEM)] * count


def call(body, outs, ins, flops=0, scalars=()):
    moved = sum(math.prod(o.shape) * o.dtype.itemsize for o in outs)
    moved += sum(math.prod(i.shape) * i.dtype.itemsize for i in ins)
    return pl.pallas_call(
        body,
        compiler_params=params,
        out_shape=outs,
        in_specs=[pl.BlockSpec(memory_space=SMEM)] * len(scalars) + vmem(len(ins)),
        out_specs=vmem(len(outs)),
        cost_estimate=pl.CostEstimate(flops=flops, bytes_accessed=moved, transcendentals=0),
    )(*scalars, *ins)


def shape(rows, cols, dtype=f32):
    return jax.ShapeDtypeStruct((rows, cols), dtype)


def local(documents, labels, skeleton, transfer, near_peer, near_live, couple_peer, couple_live):
    size = lax.axis_size("doc")
    place = jnp.reshape(lax.axis_index("doc"), (1,)).astype(jnp.int32)
    docs, width = documents.shape
    cols = labels.shape[1]
    rank = skeleton.shape[0]
    kept = cols + 8
    tall = cols + 16

    sums = [shape(tall, rank), shape(tall, rank, bf16)]
    products = [shape(kept, rank), shape(tall, rank, bf16)]
    square = shape(rank, rank)
    split = docs - step
    smem = pl.BlockSpec(memory_space=SMEM)
    hbm = pl.BlockSpec(memory_space=pltpu.HBM)

    mid_points = shift_by(skeleton, -4)
    outs = pl.pallas_call(
        functools.partial(leaf_kernel, size),
        name="leaf",
        compiler_params=params,
        out_shape=[
            jax.ShapeDtypeStruct((2 * (1 + couple_peer.shape[1]),), f32),
            shape(docs, width, bf16),
            shape(8, docs),
            shape(rank, width, bf16),
            shape(8, rank),
            shape(docs, rank, bf16),
            shape(tall, docs + rank, bf16),
        ]
        + sums
        + [square, square, shape(split, width, bf16), shape(docs - split, width, bf16)],
        in_specs=[smem] + [hbm] * 8,
        out_specs=[smem] + vmem(12),
        scratch_shapes=[
            VMEM((rank, width), bf16),
            VMEM((docs, cols), bf16),
            SMEM(near_peer.shape, jnp.int32),
            SMEM(near_peer.shape, jnp.int32),
            SMEM(couple_peer.shape[:0:-1], jnp.int32),
            SMEM(couple_peer.shape[:0:-1], jnp.int32),
            pltpu.SemaphoreType.DMA((8 + docs // step,)),
        ],
        cost_estimate=pl.CostEstimate(
            flops=2 * docs * rank * width, bytes_accessed=4 << 20, transcendentals=0
        ),
    )(place, in_hbm(near_peer), in_hbm(near_live), in_hbm(slots_first(couple_peer)), in_hbm(slots_first(couple_live)), in_hbm(transfer), in_hbm(documents), in_hbm(skeleton), in_hbm(labels))
    counts, rows, row, points, prow, leaf, across, lifted, lifted_sent = outs[:9]
    low_move, high_move, first_docs, last_docs = outs[9:]
    lifted, lifted_sent = call(add_kernel, sums, (lifted, partner(lifted_sent, 0)))
    sent_mid, lifted, lifted_sent = call(
        take_kernel, [shape(tall, rank, bf16)] + sums, (lifted, partner(lifted_sent, 1), high_move)
    )
    other_low = shift_by(skeleton, 1)
    first_docs = shift_by(first_docs, 1)
    last_docs = shift_by(last_docs, 1)
    other_labels = shift_by(across, 1)
    top_points = routed(skeleton, top_routes(size))
    (own,) = call(
        own_kernel, [shape(kept, docs)], (rows, row, across), flops=2 * docs * docs * width
    )
    (top,) = call(top_kernel, [shape(tall, rank, bf16)], (lifted, partner(lifted_sent, 2)))
    top_before, top_after = swap(top, 16)
    paired = top_before is top_after
    cross_before, cross_after = swap_cross(top, 16, 3)
    other_mid = shift_by(sent_mid, -4)
    gram = [shape(rank, rank, bf16)]
    low_gram, low_give = call(
        functools.partial(low_kernel, docs),
        gram + [shape(tall, rank, bf16)],
        (points, prow, across, other_low),
    )
    (mid_gram,) = call(gram_kernel, gram, (points, prow, mid_points))
    (top_gram,) = call(gram_kernel, gram, (points, prow, top_points))
    top_back = routed(top_gram, [(j, i) for i, j in top_routes(size)])
    mid_mine, mid_give = call(couple_kernel, products, (mid_gram, sent_mid, other_mid))
    mid_back = shift_by(mid_give, 4)
    shared = (rows, row, across)
    first_tile, first_back = call(
        tile_kernel,
        [shape(docs, split, bf16), shape(tall, split + rank, bf16)],
        (*shared, first_docs, low_give),
        flops=2 * docs * split * width,
    )
    last_tile, last_back = call(
        tile_kernel,
        [shape(docs, docs - split, bf16), shape(tall, docs - split, bf16)],
        (*shared, last_docs),
        flops=2 * docs * (docs - split) * width,
    )
    first_back = shift_by(first_back, -1)
    last_back = shift_by(last_back, -1)
    (part,) = call(
        functools.partial(far_kernel, paired),
        [shape(kept, docs)],
        (
            low_move,
            high_move,
            top_gram,
            top_back,
            top_before,
            cross_before,
            top_after,
            cross_after,
            mid_mine,
            mid_back,
            leaf,
            own,
        ),
        scalars=(counts, goes_down(place).astype(jnp.int32)),
    )
    return pl.pallas_call(
        score_kernel,
        name="score",
        compiler_params=params,
        out_shape=shape(docs, cols),
        in_specs=[smem] + vmem(8),
        out_specs=hbm,
        scratch_shapes=[VMEM((docs, cols), f32), pltpu.SemaphoreType.DMA((docs // step,))],
        cost_estimate=pl.CostEstimate(
            flops=4 * docs * docs * cols, bytes_accessed=4 << 20, transcendentals=0
        ),
    )(counts, part, leaf, low_gram, other_labels, first_tile, last_tile, first_back, last_back)


def solution(mesh):
    placed = (
        P("doc", None),
        P("doc", None),
        P("doc", None),
        P(),
        P("doc", None),
        P("doc", None),
        P("doc", None, None),
        P("doc", None, None),
    )
    return jax.shard_map(
        local, mesh=mesh, in_specs=placed, out_specs=P("doc", None), check_vma=False
    )
```
